32 devices in a mesh: groups: 2 (over x), dp: 16 (over z, y, core).
Axes of the slice: x: 2, y: 2, z: 4, core: 2. Of those that a mesh axis runs over, the one named last changes fastest.
Arguments:
- embeddings: bfloat16 [4096, 1024], P(('groups', 'dp')), parts along dimension 0
- cluster_ids: int32 [4096], P(('groups', 'dp')), parts along dimension 0, may hold values from 0 to 511, as said below
- owner: int32 [1024], P('groups'), parts along dimension 0, may hold values from 0 to 15, as said below
Outputs:
- smoothed: bfloat16 [4096, 1024], P(('groups', 'dp')), parts along dimension 0
The draws below stay inside these ranges and needn't reach their ends.
There are 2 independent parts, one for each index of `groups`. The reference program is written for one: setup_inputs(seed, part) draws one part's arguments, and reference() takes and returns one part's arrays. A program takes and returns all parts, laid end to end along the dimension named above; each array names one. Nothing has to cross between parts.
Inputs may be any that keep to these rules, and one draw needn't show every extreme that they name: `owner`: every device number owns exactly 32 clusters. `cluster_ids`: among the rows of one device, at most 16 belong to clusters of one owner, and on every device some owner gets exactly 16 of them.
All inputs are finite; a program needn't handle non-finite values.
Results may differ from the reference program's by a relative error of at most 0.0041.
Values may be sent and summed in bfloat16 or wider, within the bound.
No kernel may reach another device: no remote copies, remote signals or barrier semaphores. Data moves between devices by JAX's collectives and lax.ppermute only.
A program may use at most 64 MiB of HBM per device.

```python
import jax
import jax.numpy as jnp
from jax import lax

D = 1024
ROW_DEV = 128
CLU_DEV = 32
CLUSTERS = 512
ROWS = 2048
SLOT = 16
N_DP = 16


def owner_perm(key):
    return jax.random.permutation(jax.random.fold_in(key, 11), CLUSTERS)


def row_clusters(key):
    perm = owner_perm(key)
    total = N_DP * SLOT
    boost = jax.random.randint(jax.random.fold_in(key, 12), (N_DP,), 0, 4) * (1 << 17)
    slot_owner = jnp.arange(total, dtype=jnp.int32) // SLOT

    def one_source(source_index):
        split_key = jax.random.fold_in(jax.random.fold_in(key, 13), source_index)
        first_block, latter_tile, third_block, fourth_block = jax.random.split(split_key, 4)
        score = jax.random.randint(first_block, (total,), 0, 1 << 18) + boost[slot_owner]
        selected_holder = jax.random.randint(latter_tile, (), 0, N_DP)
        score = jnp.where(slot_owner == selected_holder, -1, score)
        chosen = jnp.argsort(score, stable=True)[:ROW_DEV]
        target = jax.random.permutation(third_block, chosen // SLOT)
        local = jax.random.randint(fourth_block, (ROW_DEV,), 0, CLU_DEV)
        return perm[target * CLU_DEV + local]
    return jax.vmap(one_source)(jnp.arange(N_DP, dtype=jnp.int32)).reshape(ROWS).astype(jnp.int32)


def draw_owner(key, part):
    return (jnp.argsort(owner_perm(key)) // CLU_DEV).astype(jnp.int32)


def draw_cluster_ids(key, part):
    return row_clusters(key)


def draw_embeddings(key, part):
    labels = row_clusters(key)
    ckey = jax.random.fold_in(key, 14)
    centers = jax.vmap(lambda label: jax.random.normal(jax.random.fold_in(ckey, label), (D,), jnp.float32))(labels)
    mkey, nkey = jax.random.split(jax.random.fold_in(key, 15), 2)
    mixing = jax.random.uniform(mkey, (ROWS, 1), jnp.float32, 0.35, 1.0)
    noise = jax.random.normal(nkey, (ROWS, D), jnp.float32)
    values = mixing * centers + jnp.sqrt(1.0 - mixing * mixing) * noise
    return values.astype(jnp.bfloat16)


def setup_inputs(seed: int = 0, part: int = 0) -> dict:
    splits = jax.random.split(jax.random.key(seed), 4)
    own_keys = jax.random.split(jax.random.fold_in(splits[3], part), 4)
    embeddings = draw_embeddings(jax.random.fold_in(jax.random.fold_in(splits[3], part), 71), part)
    cluster_ids = draw_cluster_ids(jax.random.fold_in(jax.random.fold_in(splits[3], part), 71), part)
    owner = draw_owner(jax.random.fold_in(jax.random.fold_in(splits[3], part), 71), part)
    return {"embeddings": embeddings, "cluster_ids": cluster_ids, "owner": owner}


epsilon = 1e-06
sharpness_scale = 0.25

def smooth_rows(rows, labels):
    values = rows.astype(jnp.float32)
    unit = (values * lax.rsqrt(lax.optimization_barrier(jnp.sum(values * values, axis=1, keepdims=True)) + epsilon)).astype(jnp.bfloat16)
    pairwise_similarity = jnp.dot(unit, unit.T, preferred_element_type=jnp.float32)
    shared_group_filter = (labels[:, None] == labels[None, :]) & (labels[:, None] >= 0)
    affinity_factor = jnp.where(shared_group_filter, jnp.exp((pairwise_similarity - 1.0) / sharpness_scale), jnp.float32(0.0))
    total = lax.optimization_barrier(jnp.sum(affinity_factor, axis=1))
    numer = jnp.dot(affinity_factor.astype(jnp.bfloat16), rows, preferred_element_type=jnp.float32)
    total = jnp.where(labels >= 0, total, jnp.float32(1.0))
    return (numer / total[:, None]).astype(jnp.bfloat16)

def reference(embeddings, cluster_ids, owner):
    dest = jnp.take(owner, cluster_ids).astype(jnp.int32)
    by_source = dest.reshape(N_DP, ROW_DEV)
    onehot = (by_source[:, :, None] == jnp.arange(N_DP, dtype=jnp.int32)[None, None, :]).astype(jnp.int32)
    rank = lax.optimization_barrier(jnp.sum(onehot * (jnp.cumsum(onehot, axis=1) - 1), axis=2)).astype(jnp.int32)
    source_index = jnp.arange(N_DP, dtype=jnp.int32)[:, None] * SLOT + rank
    table = jnp.full((N_DP, N_DP * SLOT), ROWS, jnp.int32)
    table = table.at[by_source.reshape(-1), source_index.reshape(-1)].set(jnp.arange(ROWS, dtype=jnp.int32))

    def per_owner(indices):
        valid = indices < ROWS
        safe = jnp.minimum(indices, ROWS - 1)
        rows = jnp.where(valid[:, None], embeddings[safe], jnp.zeros((), jnp.bfloat16))
        labels = jnp.where(valid, cluster_ids[safe], -1).astype(jnp.int32)
        return smooth_rows(rows, labels)
    results = lax.map(per_owner, table)
    output = jnp.zeros((ROWS, D), jnp.bfloat16)
    return output.at[table.reshape(-1)].set(results.reshape(-1, D), mode='drop')
```

```python
import jax
import jax.numpy as jnp
from jax import lax
from jax.experimental import pallas as pl
from jax.experimental.pallas import tpu as pltpu
from jax.sharding import PartitionSpec as P

epsilon = 1e-06
sharpness_scale = 0.25
pad = 8


def normalize(rows):
    values = rows.astype(jnp.float32)
    return (values * lax.rsqrt(jnp.sum(values * values, axis=1, keepdims=True) + epsilon)).astype(
        jnp.bfloat16
    )


def kernel_terms(query_unit, query_labels, key_unit, compared_group_ids, key_rows):
    pairwise_similarity = jnp.dot(query_unit, key_unit.T, preferred_element_type=jnp.float32)
    shared_group_filter = (query_labels[:, None] == compared_group_ids[None, :]) & (
        query_labels[:, None] >= 0
    )
    affinity_factor = jnp.where(
        shared_group_filter,
        jnp.exp((pairwise_similarity - 1.0) / sharpness_scale),
        jnp.float32(0.0),
    )
    total = jnp.sum(affinity_factor, axis=1)
    numer = jnp.dot(
        affinity_factor.astype(jnp.bfloat16), key_rows, preferred_element_type=jnp.float32
    )
    return (numer, total)


def finish(numer, total, labels):
    total = jnp.where(labels >= 0, total, jnp.float32(1.0))
    return (numer / total[:, None]).astype(jnp.bfloat16)


def exchange(embeddings, cluster_ids, owner):
    peers = lax.axis_size("dp")
    rows_dev, width = embeddings.shape
    slot = 2 * rows_dev // peers
    dest = jnp.take(owner, cluster_ids)
    onehot = (dest[:, None] == jnp.arange(peers, dtype=jnp.int32)[None, :]).astype(jnp.int32)
    rank = jnp.sum(onehot * (jnp.cumsum(onehot, axis=0) - 1), axis=1)
    target = dest * slot + rank
    outgoing = (
        jnp.zeros((peers * slot, width), jnp.bfloat16)
        .at[target]
        .set(embeddings)
        .reshape(peers, slot, width)
    )
    labels = (
        jnp.full((peers * slot,), -1, jnp.int32).at[target].set(cluster_ids).reshape(peers, slot)
    )
    received, got_labels = (
        lax.all_to_all(outgoing, "dp", split_axis=0, concat_axis=0, tiled=True),
        lax.all_to_all(labels, "dp", split_axis=0, concat_axis=0, tiled=True),
    )
    flat_rows = received.reshape(-1, width)
    flat_labels = got_labels.reshape(-1)
    unit = normalize(flat_rows)
    numer, total = kernel_terms(unit, flat_labels, unit, flat_labels, flat_rows)
    result = finish(numer, total, flat_labels).reshape(peers, slot, width)
    back = lax.all_to_all(result, "dp", split_axis=0, concat_axis=0, tiled=True)
    return back.reshape(-1, width)[target]


LAYERS, COLUMNS, CORES = 4, 2, 2
NEXT = (1, 3, 0, 2)
BACK = (2, 0, 3, 1)
STAY = (0, 1, 2, 3)


def moves(layers, column, core):
    return [
        (
            (z * COLUMNS + y) * CORES + c,
            (layers[z] * COLUMNS + (y ^ column)) * CORES + (c ^ core),
        )
        for z in range(LAYERS)
        for y in range(COLUMNS)
        for c in range(CORES)
    ]


def row_ids(ids_ref, at):
    return ids_ref[pl.ds(at, 1), :].astype(jnp.float32)


def column_ids(ids_ref, at):
    row = row_ids(ids_ref, at)
    n = row.shape[1]
    return jnp.transpose(jnp.broadcast_to(row, (n, n)))


def partial_sums(unit, ids, keys):
    numer, total = None, None
    for key_unit, key_ids, key_rows in keys:
        gram = lax.dot_general(
            unit, key_unit, (((1,), (1,)), ((), ())), preferred_element_type=jnp.float32
        )
        weight = jnp.where(ids == key_ids, jnp.exp((gram - 1.0) / sharpness_scale), 0.0)
        part = jnp.sum(weight, axis=1, keepdims=True)
        sums = jnp.dot(
            weight.astype(jnp.bfloat16), key_rows, preferred_element_type=jnp.float32
        )
        total = part if total is None else total + part
        numer = sums if numer is None else numer + sums
    return numer, total


def store_partial(out_ref, numer, total):
    n, width = numer.shape
    out_ref[:n, :] = numer.astype(jnp.bfloat16)
    row = jnp.transpose(jnp.broadcast_to(total, (n, n)))[:pad, :]
    high = row.astype(jnp.bfloat16)
    rest = row - high.astype(jnp.float32)
    middle = rest.astype(jnp.bfloat16)
    low = (rest - middle.astype(jnp.float32)).astype(jnp.bfloat16)
    out_ref[n:, :] = jnp.zeros((pad, width), jnp.bfloat16)
    out_ref[n:, :n] = high
    out_ref[n:, n : 2 * n] = middle
    out_ref[n:, 2 * n : 3 * n] = low


def load_total(ref, n):
    parts = ref[n:, : 3 * n].astype(jnp.float32)
    row = parts[:1, :n] + parts[:1, n : 2 * n] + parts[:1, 2 * n : 3 * n]
    return jnp.transpose(jnp.broadcast_to(row, (n, n)))[:, :1]


def early_body(at, ids, own, own2, col, col2, ring, ring2, numer, total, unit, side, side_total, back):
    rows = [own[...], own2[...], col[...], col2[...], ring[...], ring2[...]]
    units = [normalize(r) for r in rows]
    keys = [(units[k], row_ids(ids, at[k]), rows[k]) for k in range(6)]
    numer[...], t = partial_sums(units[0], column_ids(ids, at[0]), keys)
    total[...] = jnp.broadcast_to(t, total.shape)
    unit[0] = units[0]
    unit[1] = units[2]
    side[...], t = partial_sums(units[2], column_ids(ids, at[2]), keys[4:])
    side_total[...] = jnp.broadcast_to(t, side_total.shape)
    store_partial(back, *partial_sums(units[4], column_ids(ids, at[4]), keys[:4]))


def side_body(at, ids, unit, side, side_total, far, far2, out, far_unit):
    rows = [far[...], far2[...]]
    units = [normalize(r) for r in rows]
    keys = [(units[k], row_ids(ids, at[6 + k]), rows[k]) for k in range(2)]
    numer, t = partial_sums(unit[1], column_ids(ids, at[2]), keys)
    store_partial(out, numer + side[...], t + side_total[:, :1])
    far_unit[0] = units[0]
    far_unit[1] = units[1]


def late_body(at, ids, unit, numer, total, far, far2, far_unit, numer_out, total_out):
    rows = [far[...], far2[...]]
    keys = [(far_unit[k], row_ids(ids, at[6 + k]), rows[k]) for k in range(2)]
    sums, t = partial_sums(unit[0], column_ids(ids, at[0]), keys)
    numer_out[...] = sums + numer[...]
    total_out[...] = jnp.broadcast_to(t, total_out.shape) + total[...]


def finish_body(numer, total, back, side, out):
    n = out.shape[0]
    t = total[:, :1] + load_total(back, n) + load_total(side, n)
    sums = numer[...] + back[:n, :].astype(jnp.float32) + side[:n, :].astype(jnp.float32)
    out[...] = (sums / t).astype(jnp.bfloat16)


def call(body, name, outs, *args, scalars=1):
    smem = pl.BlockSpec(memory_space=pltpu.SMEM)
    vmem = pl.BlockSpec(memory_space=pltpu.VMEM)
    return pl.pallas_call(
        body,
        name=name,
        out_shape=[jax.ShapeDtypeStruct(shape, dtype) for shape, dtype in outs],
        in_specs=[smem] * scalars + [vmem] * (len(args) - scalars),
        out_specs=[vmem] * len(outs),
    )(*args)


def gathered(embeddings, cluster_ids):
    n, width = embeddings.shape
    peers = LAYERS * COLUMNS * CORES

    def send(rows, layers, column, core):
        return lax.ppermute(rows, "dp", moves(layers, column, core))

    ring = send(embeddings, NEXT, 0, 0)
    col = send(embeddings, STAY, 1, 0)
    own2 = send(embeddings, STAY, 0, 1)
    ids = lax.all_to_all(
        jnp.broadcast_to(cluster_ids[None, :], (peers, n)), "dp", 0, 0, tiled=True
    )
    far = send(ring, NEXT, 0, 0)
    col2 = send(col, STAY, 0, 1)
    ring2 = send(ring, STAY, 0, 1)
    far2 = send(far, STAY, 0, 1)

    me = lax.axis_index("dp")
    per = COLUMNS * CORES
    back_of = jnp.array(BACK, jnp.int32)
    layer, place = me // per, me % per
    before = back_of[layer]
    before2 = LAYERS - 1 - layer
    at = jnp.stack(
        [
            me,
            me ^ 1,
            me ^ 2,
            me ^ 3,
            before * per + place,
            before * per + (place ^ 1),
            before2 * per + place,
            before2 * per + (place ^ 1),
        ]
    ).astype(jnp.int32)

    f32, bf16 = jnp.float32, jnp.bfloat16
    sums, lanes = ((n, width), f32), ((n, n), f32)
    packet = ((n + pad, width), bf16)
    numer, total, unit, side, side_total, back = call(
        early_body,
        "early",
        [sums, lanes, ((2, n, width), bf16), sums, lanes, packet],
        at, ids, embeddings, own2, col, col2, ring, ring2,
    )
    back = send(back, BACK, 0, 0)
    side, far_unit = call(
        side_body, "side", [packet, ((2, n, width), bf16)], at, ids, unit, side, side_total, far, far2
    )
    side = send(side, STAY, 1, 0)
    numer, total = call(
        late_body, "late", [sums, lanes], at, ids, unit, numer, total, far, far2, far_unit
    )
    return call(
        finish_body, "finish", [((n, width), bf16)], numer, total, back, side, scalars=0
    )[0]


def shards(embeddings, cluster_ids, owner):
    if lax.axis_size("dp") == LAYERS * COLUMNS * CORES:
        return gathered(embeddings, cluster_ids)
    return exchange(embeddings, cluster_ids, owner)


def solution(mesh):
    placed = (P(("groups", "dp"), None), P(("groups", "dp")), P("groups"))
    return jax.shard_map(
        shards, mesh=mesh, in_specs=placed, out_specs=P(("groups", "dp"), None), check_vma=False
    )
```

```python
import jax
import jax.numpy as jnp
from jax import lax
from jax.experimental import pallas as pl
from jax.experimental.pallas import tpu as pltpu
from jax.sharding import PartitionSpec as P


epsilon = 1e-06
sharpness_scale = 0.25
pad = 8


def normalize(rows):
    values = rows.astype(jnp.float32)
    return (values * lax.rsqrt(jnp.sum(values * values, axis=1, keepdims=True) + epsilon)).astype(
        jnp.bfloat16
    )


def kernel_terms(query_unit, query_labels, key_unit, compared_group_ids, key_rows):
    pairwise_similarity = jnp.dot(query_unit, key_unit.T, preferred_element_type=jnp.float32)
    shared_group_filter = (query_labels[:, None] == compared_group_ids[None, :]) & (
        query_labels[:, None] >= 0
    )
    affinity_factor = jnp.where(
        shared_group_filter,
        jnp.exp((pairwise_similarity - 1.0) / sharpness_scale),
        jnp.float32(0.0),
    )
    total = jnp.sum(affinity_factor, axis=1)
    numer = jnp.dot(
        affinity_factor.astype(jnp.bfloat16), key_rows, preferred_element_type=jnp.float32
    )
    return (numer, total)


def finish(numer, total, labels):
    total = jnp.where(labels >= 0, total, jnp.float32(1.0))
    return (numer / total[:, None]).astype(jnp.bfloat16)


def exchange(embeddings, cluster_ids, owner):
    peers = lax.axis_size("dp")
    rows_dev, width = embeddings.shape
    slot = 2 * rows_dev // peers
    dest = jnp.take(owner, cluster_ids)
    onehot = (dest[:, None] == jnp.arange(peers, dtype=jnp.int32)[None, :]).astype(jnp.int32)
    rank = jnp.sum(onehot * (jnp.cumsum(onehot, axis=0) - 1), axis=1)
    target = dest * slot + rank
    outgoing = (
        jnp.zeros((peers * slot, width), jnp.bfloat16)
        .at[target]
        .set(embeddings)
        .reshape(peers, slot, width)
    )
    labels = (
        jnp.full((peers * slot,), -1, jnp.int32).at[target].set(cluster_ids).reshape(peers, slot)
    )
    received, got_labels = (
        lax.all_to_all(outgoing, "dp", split_axis=0, concat_axis=0, tiled=True),
        lax.all_to_all(labels, "dp", split_axis=0, concat_axis=0, tiled=True),
    )
    flat_rows = received.reshape(-1, width)
    flat_labels = got_labels.reshape(-1)
    unit = normalize(flat_rows)
    numer, total = kernel_terms(unit, flat_labels, unit, flat_labels, flat_rows)
    result = finish(numer, total, flat_labels).reshape(peers, slot, width)
    back = lax.all_to_all(result, "dp", split_axis=0, concat_axis=0, tiled=True)
    return back.reshape(-1, width)[target]


LAYERS, COLUMNS, CORES = 4, 2, 2
NEXT = (1, 3, 0, 2)
BACK = (2, 0, 3, 1)
STAY = (0, 1, 2, 3)


def moves(layers, column, core):
    return [
        (
            (z * COLUMNS + y) * CORES + c,
            (layers[z] * COLUMNS + (y ^ column)) * CORES + (c ^ core),
        )
        for z in range(LAYERS)
        for y in range(COLUMNS)
        for c in range(CORES)
    ]


def store_row(out_ref, n, row):
    high = row.astype(jnp.bfloat16)
    rest = row - high.astype(jnp.float32)
    middle = rest.astype(jnp.bfloat16)
    low = (rest - middle.astype(jnp.float32)).astype(jnp.bfloat16)
    out_ref[n:, :] = jnp.zeros((pad, out_ref.shape[1]), jnp.bfloat16)
    out_ref[n:, :n] = high
    out_ref[n:, n : 2 * n] = middle
    out_ref[n:, 2 * n : 3 * n] = low


def load_row(ref, n):
    parts = ref[n:, : 3 * n].astype(jnp.float32)
    return parts[:1, :n] + parts[:1, n : 2 * n] + parts[:1, 2 * n : 3 * n]


def as_column(row):
    n = row.shape[1]
    return jnp.transpose(jnp.broadcast_to(row, (n, n)))[:, :1]


def as_rows(column):
    n = column.shape[0]
    return jnp.transpose(jnp.broadcast_to(column, (n, n)))[:pad, :]


def cat(values, axis=0):
    return jnp.concatenate(values, axis=axis)


def partial_sums(units, ids, key_units, key_ids, key_rows):
    gram = lax.dot_general(
        units, key_units, (((1,), (1,)), ((), ())), preferred_element_type=jnp.float32
    )
    weight = jnp.where(ids == key_ids, jnp.exp((gram - 1.0) / sharpness_scale), 0.0)
    total = jnp.sum(weight, axis=1, keepdims=True)
    numer = jnp.dot(weight.astype(jnp.bfloat16), key_rows, preferred_element_type=jnp.float32)
    return numer, total


def pair_ids(ref):
    values = ref[...].astype(jnp.float32)
    return [values[:1], values[1:2]]


def early_body(
    own, own2, col, col2, ring, ring2, own_ids, col_ids, ring_ids, unit, sums, totals, back
):
    n = own.shape[0]
    rows = [ref[...] for ref in (own, own2, col, col2, ring, ring2)]
    ids = pair_ids(own_ids) + pair_ids(col_ids) + pair_ids(ring_ids)
    units = [normalize(r) for r in rows]
    of_own, of_col, of_ring = as_column(ids[0]), as_column(ids[2]), as_column(ids[4])
    numer, total = partial_sums(
        cat([units[0], units[4]]), cat([of_own, of_ring]), cat(units[:4]), cat(ids[:4], 1), cat(rows[:4])
    )
    back[:n, :] = numer[n:].astype(jnp.bfloat16)
    store_row(back, n, as_rows(total[n:]))
    pair = cat([units[0], units[2]])
    numer2, total2 = partial_sums(
        pair, cat([of_own, of_col]), cat(units[4:]), cat(ids[4:], 1), cat(rows[4:])
    )
    unit[...] = pair
    sums[:n, :] = numer[:n] + numer2[:n]
    sums[n:, :] = numer2[n:]
    totals[:n, :] = jnp.broadcast_to(total[:n] + total2[:n], (n, n))
    totals[n:, :] = jnp.broadcast_to(total2[n:], (n, n))


def side_body(own_ids, col_ids, far_ids, unit, sums, totals, far, far2, numer, total, side):
    n = far.shape[0]
    rows = [far[...], far2[...]]
    mine = cat([as_column(pair_ids(own_ids)[0]), as_column(pair_ids(col_ids)[0])])
    part, t = partial_sums(
        unit[...], mine, cat([normalize(r) for r in rows]), cat(pair_ids(far_ids), 1), cat(rows)
    )
    side[:n, :] = (part[n:] + sums[n:, :]).astype(jnp.bfloat16)
    store_row(side, n, as_rows(t[n:] + totals[n:, :1]))
    numer[...] = part[:n] + sums[:n, :]
    total[...] = t[:n] + totals[:n, :]


def finish_body(numer, total, back, side, out):
    n = out.shape[0]
    t = total[:, :1] + as_column(load_row(back, n)) + as_column(load_row(side, n))
    sums = numer[...] + back[:n, :].astype(jnp.float32) + side[:n, :].astype(jnp.float32)
    out[...] = (sums / t).astype(jnp.bfloat16)


def call(body, outs, *args, close=True):
    vmem = pl.BlockSpec(memory_space=pltpu.VMEM)
    if close:
        kinds = [pltpu.VMEM(shape, dtype) for shape, dtype in outs]
    else:
        kinds = [jax.ShapeDtypeStruct(shape, dtype) for shape, dtype in outs]
    return pl.pallas_call(
        body,
        out_shape=kinds,
        in_specs=[vmem] * len(args),
        out_specs=[vmem] * len(outs),
        compiler_params=pltpu.CompilerParams(vmem_limit_bytes=24 * 2**20),
    )(*args)


def near(*arrays):
    return [pltpu.with_memory_space_constraint(x, pltpu.VMEM) for x in arrays]


def gathered(embeddings, cluster_ids):
    n, width = embeddings.shape

    def send(rows, layers, column, core):
        return lax.ppermute(rows, "dp", moves(layers, column, core))

    f32, bf16 = jnp.float32, jnp.bfloat16
    packet = ((n + pad, width), bf16)
    own = embeddings
    ring = send(own, NEXT, 0, 0)
    col = send(own, STAY, 1, 0)
    own2 = send(own, STAY, 0, 1)
    one = cluster_ids[None, :]
    own_ids = cat([one, send(one, STAY, 0, 1)])
    ring_ids = send(own_ids, NEXT, 0, 0)
    col_ids = send(own_ids, STAY, 1, 0)
    far = send(ring, NEXT, 0, 0)
    far_ids = send(ring_ids, NEXT, 0, 0)
    col2 = send(col, STAY, 0, 1)
    ring2 = send(ring, STAY, 0, 1)

    unit, sums, totals, back = call(
        early_body,
        [((2 * n, width), bf16), ((2 * n, width), f32), ((2 * n, n), f32), packet],
        *near(own, own2, col, col2, ring, ring2, own_ids, col_ids, ring_ids),
    )
    back = send(back, BACK, 0, 0)
    far, sums = lax.optimization_barrier((far, sums))
    far2 = send(far, STAY, 0, 1)
    numer, total, side = call(
        side_body,
        [((n, width), f32), ((n, n), f32), packet],
        *near(own_ids, col_ids, far_ids, unit, sums, totals, far, far2),
    )
    side = send(side, STAY, 1, 0)
    return call(finish_body, [((n, width), bf16)], *near(numer, total, back, side), close=False)[0]


def shards(embeddings, cluster_ids, owner):
    if lax.axis_size("dp") == LAYERS * COLUMNS * CORES:
        return gathered(embeddings, cluster_ids)
    return exchange(embeddings, cluster_ids, owner)


def solution(mesh):
    placed = (P(("groups", "dp"), None), P(("groups", "dp")), P("groups"))
    return jax.shard_map(
        shards, mesh=mesh, in_specs=placed, out_specs=P(("groups", "dp"), None), check_vma=False
    )
```

```python
import jax
import jax.numpy as jnp
from jax import lax
from jax.experimental import pallas as pl
from jax.experimental.pallas import tpu as pltpu
from jax.sharding import PartitionSpec as P


epsilon = 1e-06
sharpness_scale = 0.25
pad = 8


def normalize(rows):
    values = rows.astype(jnp.float32)
    return (values * lax.rsqrt(jnp.sum(values * values, axis=1, keepdims=True) + epsilon)).astype(
        jnp.bfloat16
    )


def kernel_terms(query_unit, query_labels, key_unit, compared_group_ids, key_rows):
    pairwise_similarity = jnp.dot(query_unit, key_unit.T, preferred_element_type=jnp.float32)
    shared_group_filter = (query_labels[:, None] == compared_group_ids[None, :]) & (
        query_labels[:, None] >= 0
    )
    affinity_factor = jnp.where(
        shared_group_filter,
        jnp.exp((pairwise_similarity - 1.0) / sharpness_scale),
        jnp.float32(0.0),
    )
    total = jnp.sum(affinity_factor, axis=1)
    numer = jnp.dot(
        affinity_factor.astype(jnp.bfloat16), key_rows, preferred_element_type=jnp.float32
    )
    return (numer, total)


def finish(numer, total, labels):
    total = jnp.where(labels >= 0, total, jnp.float32(1.0))
    return (numer / total[:, None]).astype(jnp.bfloat16)


def exchange(embeddings, cluster_ids, owner):
    peers = lax.axis_size("dp")
    rows_dev, width = embeddings.shape
    slot = 2 * rows_dev // peers
    dest = jnp.take(owner, cluster_ids)
    onehot = (dest[:, None] == jnp.arange(peers, dtype=jnp.int32)[None, :]).astype(jnp.int32)
    rank = jnp.sum(onehot * (jnp.cumsum(onehot, axis=0) - 1), axis=1)
    target = dest * slot + rank
    outgoing = (
        jnp.zeros((peers * slot, width), jnp.bfloat16)
        .at[target]
        .set(embeddings)
        .reshape(peers, slot, width)
    )
    labels = (
        jnp.full((peers * slot,), -1, jnp.int32).at[target].set(cluster_ids).reshape(peers, slot)
    )
    received, got_labels = (
        lax.all_to_all(outgoing, "dp", split_axis=0, concat_axis=0, tiled=True),
        lax.all_to_all(labels, "dp", split_axis=0, concat_axis=0, tiled=True),
    )
    flat_rows = received.reshape(-1, width)
    flat_labels = got_labels.reshape(-1)
    unit = normalize(flat_rows)
    numer, total = kernel_terms(unit, flat_labels, unit, flat_labels, flat_rows)
    result = finish(numer, total, flat_labels).reshape(peers, slot, width)
    back = lax.all_to_all(result, "dp", split_axis=0, concat_axis=0, tiled=True)
    return back.reshape(-1, width)[target]


LAYERS, COLUMNS, CORES = 4, 2, 2
NEXT = (1, 3, 0, 2)
BACK = (2, 0, 3, 1)
STAY = (0, 1, 2, 3)


def moves(layers, column, core):
    return [
        (
            (z * COLUMNS + y) * CORES + c,
            (layers[z] * COLUMNS + (y ^ column)) * CORES + (c ^ core),
        )
        for z in range(LAYERS)
        for y in range(COLUMNS)
        for c in range(CORES)
    ]


def store_row(out_ref, n, at, row):
    high = row.astype(jnp.bfloat16)
    rest = row - high.astype(jnp.float32)
    middle = rest.astype(jnp.bfloat16)
    low = (rest - middle.astype(jnp.float32)).astype(jnp.bfloat16)
    out_ref[at:, :] = jnp.zeros((pad, out_ref.shape[1]), jnp.bfloat16)
    out_ref[at:, :n] = high
    out_ref[at:, n : 2 * n] = middle
    out_ref[at:, 2 * n : 3 * n] = low


def load_row(ref, n):
    at = ref.shape[0] - pad
    parts = ref[at:, : 3 * n].astype(jnp.float32)
    return parts[:1, :n] + parts[:1, n : 2 * n] + parts[:1, 2 * n : 3 * n]


def as_column(row):
    n = row.shape[1]
    return jnp.transpose(jnp.broadcast_to(row, (n, n)))[:, :1]


def as_rows(column):
    n = column.shape[0]
    return jnp.transpose(jnp.broadcast_to(column, (n, n)))[:pad, :]


def cat(values, axis=0):
    return jnp.concatenate(values, axis=axis)


def weights(units, ids, key_units, key_ids):
    gram = lax.dot_general(
        units, key_units, (((1,), (1,)), ((), ())), preferred_element_type=jnp.float32
    )
    weight = jnp.where(ids == key_ids, jnp.exp((gram - 1.0) / sharpness_scale), 0.0)
    return weight.astype(jnp.bfloat16), jnp.sum(weight, axis=1, keepdims=True)


def weighted(weight, rows):
    return jnp.dot(weight, rows, preferred_element_type=jnp.float32)


def join_body(rows, ids, out):
    n = rows.shape[0]
    out[:n, :] = rows[...]
    store_row(out, n, n, jnp.broadcast_to(ids[...].astype(jnp.float32), (pad, n)))


def split_body(rows, ids, out, first, second):
    n = rows.shape[0]
    half = n // 2
    row = jnp.broadcast_to(ids[...].astype(jnp.float32), (pad, n))
    out[:n, :] = rows[...]
    store_row(out, n, n, row)
    first[:half, :] = rows[:half, :]
    store_row(first, n, half, row)
    second[...] = rows[half:, :]


def early_body(own, own2, col, col2, ring, ring2, own_ids, own2_ids, unit, sums, totals, back):
    n = own.shape[0]
    blocks = (col, col2, ring, ring2)
    rows = [own[...], own2[...]] + [ref[:n, :] for ref in blocks]
    ids = [ref[...].astype(jnp.float32) for ref in (own_ids, own2_ids)]
    ids += [load_row(ref, n) for ref in blocks]
    units = [normalize(r) for r in rows]
    of_own, of_ring = as_column(ids[0]), as_column(ids[4])
    weight, total = weights(
        cat([units[0], units[4]]), cat([of_own, of_ring]), cat(units[:4]), cat(ids[:4], 1)
    )
    numer = weighted(weight, cat(rows[:4]))
    back[:n, :] = numer[n:].astype(jnp.bfloat16)
    store_row(back, n, n, as_rows(total[n:]))
    weight2, total2 = weights(units[0], of_own, cat(units[4:]), cat(ids[4:], 1))
    unit[...] = units[0]
    sums[...] = numer[:n] + weighted(weight2, cat(rows[4:]))
    totals[...] = jnp.broadcast_to(total[:n] + total2, (n, n))


def key_sums(unit, ids, keys):
    rows = cat([row for row, _ in keys])
    weight, total = weights(
        unit[...], as_column(ids[...].astype(jnp.float32)), cat([normalize(row) for row, _ in keys]),
        cat([row for _, row in keys], 1),
    )
    return weighted(weight, rows), total


def keys_of(ref, n):
    return ref[:n, :], load_row(ref, n)


def first_of(ref, n):
    return ref[: n // 2, :], load_row(ref, n)[:, : n // 2]


def second_of(ref, first, n):
    return ref[...], load_row(first, n)[:, n // 2 :]


def add_to(sums, totals, new_sums, new_totals, unit, ids, keys):
    numer, total = key_sums(unit, ids, keys)
    new_sums[...] = sums[...] + numer
    new_totals[...] = totals[...] + total


def mid_body(unit, ids, sums, totals, side, side2, fa, fa2, new_sums, new_totals):
    n = unit.shape[0]
    keys = [keys_of(side, n), keys_of(side2, n), first_of(fa, n), first_of(fa2, n)]
    add_to(sums, totals, new_sums, new_totals, unit, ids, keys)


def late_body(unit, ids, sums, totals, fa, fa2, fb, fb2, sa, sb, new_sums, new_totals):
    n = unit.shape[0]
    keys = [second_of(fb, fa, n), second_of(fb2, fa2, n), first_of(sa, n), second_of(sb, sa, n)]
    add_to(sums, totals, new_sums, new_totals, unit, ids, keys)


def finish_body(unit, ids, sums, totals, sa2, sb2, back, out, near_out, sems):
    n = unit.shape[0]
    numer, total = key_sums(unit, ids, [first_of(sa2, n), second_of(sb2, sa2, n)])
    scale = 1.0 / (total + totals[:, :1] + as_column(load_row(back, n)))
    step = n // 4
    copies = []
    for k in range(4):
        at = slice(k * step, (k + 1) * step)
        near_out[at, :] = (
            (numer[at] + sums[at, :] + back[at, :].astype(jnp.float32)) * scale[at]
        ).astype(jnp.bfloat16)
        here = pl.ds(k * step, step)
        copies.append(pltpu.make_async_copy(near_out.at[here], out.at[here], sems.at[k]))
        copies[-1].start()
    for copy in copies:
        copy.wait()


def call(body, outs, *args, out_space=pltpu.VMEM, scratch=()):
    vmem = pl.BlockSpec(memory_space=pltpu.VMEM)
    kind = pltpu.VMEM if out_space is pltpu.VMEM else jax.ShapeDtypeStruct
    return pl.pallas_call(
        body,
        out_shape=[kind(shape, dtype) for shape, dtype in outs],
        in_specs=[vmem] * len(args),
        out_specs=[pl.BlockSpec(memory_space=out_space)] * len(outs),
        scratch_shapes=scratch,
        compiler_params=pltpu.CompilerParams(vmem_limit_bytes=24 * 2**20),
    )(*args)


def near(*arrays):
    return [pltpu.with_memory_space_constraint(x, pltpu.VMEM) for x in arrays]


def gathered(embeddings, cluster_ids):
    n, width = embeddings.shape
    half = n // 2
    f32, bf16 = jnp.float32, jnp.bfloat16

    def send(rows, layers, column, core):
        return lax.ppermute(rows, "dp", moves(layers, column, core))

    def swap(rows):
        return send(rows, STAY, 0, 1)

    def join(rows, ids):
        return call(join_body, [packet], *near(rows, ids))[0]

    packet = ((n + pad, width), bf16)
    own, ids = embeddings, cluster_ids[None, :]
    ring = send(own, NEXT, 0, 0)
    ring_ids = send(ids, NEXT, 0, 0)
    col = send(own, STAY, 1, 0)
    col_ids = send(ids, STAY, 1, 0)
    own2 = swap(own)
    own2_ids = swap(ids)
    packet1, packet2 = ((half + pad, width), bf16), ((half, width), bf16)
    ring, ra, rb = call(split_body, [packet, packet1, packet2], *near(ring, ring_ids))
    fa = send(ra, NEXT, 0, 0)
    side = send(ring, STAY, 1, 0)
    ring2 = swap(ring)
    fb = send(rb, NEXT, 0, 0)
    col = join(col, col_ids)
    col2 = swap(col)

    state = [((n, width), f32), ((n, n), f32)]
    unit, sums, totals, back = call(
        early_body,
        [((n, width), bf16)] + state + [packet],
        *near(own, own2, col, col2, ring, ring2, ids, own2_ids),
    )
    fa, sums = lax.optimization_barrier((fa, sums))
    sa = send(fa, STAY, 1, 0)
    fa2 = swap(fa)
    back = send(back, BACK, 0, 0)
    sb = send(fb, STAY, 1, 0)
    fb2 = swap(fb)
    side2 = swap(side)
    fb, side2 = lax.optimization_barrier((fb, side2))
    sums, totals = call(mid_body, state, *near(unit, ids, sums, totals, side, side2, fa, fa2))
    sa, totals = lax.optimization_barrier((sa, totals))
    sa2 = swap(sa)
    sb2 = swap(sb)
    sums, totals = call(late_body, state, *near(unit, ids, sums, totals, fa, fa2, fb, fb2, sa, sb))
    out = ((n, width), bf16)
    return call(
        finish_body, [out], *near(unit, ids, sums, totals, sa2, sb2, back),
        out_space=pl.ANY, scratch=[pltpu.VMEM(*out), pltpu.SemaphoreType.DMA((4,))],
    )[0]


def shards(embeddings, cluster_ids, owner):
    if lax.axis_size("dp") == LAYERS * COLUMNS * CORES:
        return gathered(embeddings, cluster_ids)
    return exchange(embeddings, cluster_ids, owner)


def solution(mesh):
    placed = (P(("groups", "dp"), None), P(("groups", "dp")), P("groups"))
    return jax.shard_map(
        shards, mesh=mesh, in_specs=placed, out_specs=P(("groups", "dp"), None), check_vma=False
    )
```

```python
import jax
import jax.numpy as jnp
from jax import lax
from jax.experimental import pallas as pl
from jax.experimental.pallas import tpu as pltpu
from jax.sharding import PartitionSpec as P


epsilon = 1e-06
sharpness_scale = 0.25
pad = 8


def normalize(rows):
    values = rows.astype(jnp.float32)
    return (values * lax.rsqrt(jnp.sum(values * values, axis=1, keepdims=True) + epsilon)).astype(
        jnp.bfloat16
    )


def kernel_terms(query_unit, query_labels, key_unit, compared_group_ids, key_rows):
    pairwise_similarity = jnp.dot(query_unit, key_unit.T, preferred_element_type=jnp.float32)
    shared_group_filter = (query_labels[:, None] == compared_group_ids[None, :]) & (
        query_labels[:, None] >= 0
    )
    affinity_factor = jnp.where(
        shared_group_filter,
        jnp.exp((pairwise_similarity - 1.0) / sharpness_scale),
        jnp.float32(0.0),
    )
    total = jnp.sum(affinity_factor, axis=1)
    numer = jnp.dot(
        affinity_factor.astype(jnp.bfloat16), key_rows, preferred_element_type=jnp.float32
    )
    return (numer, total)


def finish(numer, total, labels):
    total = jnp.where(labels >= 0, total, jnp.float32(1.0))
    return (numer / total[:, None]).astype(jnp.bfloat16)


def exchange(embeddings, cluster_ids, owner):
    peers = lax.axis_size("dp")
    rows_dev, width = embeddings.shape
    slot = 2 * rows_dev // peers
    dest = jnp.take(owner, cluster_ids)
    onehot = (dest[:, None] == jnp.arange(peers, dtype=jnp.int32)[None, :]).astype(jnp.int32)
    rank = jnp.sum(onehot * (jnp.cumsum(onehot, axis=0) - 1), axis=1)
    target = dest * slot + rank
    outgoing = (
        jnp.zeros((peers * slot, width), jnp.bfloat16)
        .at[target]
        .set(embeddings)
        .reshape(peers, slot, width)
    )
    labels = (
        jnp.full((peers * slot,), -1, jnp.int32).at[target].set(cluster_ids).reshape(peers, slot)
    )
    received, got_labels = (
        lax.all_to_all(outgoing, "dp", split_axis=0, concat_axis=0, tiled=True),
        lax.all_to_all(labels, "dp", split_axis=0, concat_axis=0, tiled=True),
    )
    flat_rows = received.reshape(-1, width)
    flat_labels = got_labels.reshape(-1)
    unit = normalize(flat_rows)
    numer, total = kernel_terms(unit, flat_labels, unit, flat_labels, flat_rows)
    result = finish(numer, total, flat_labels).reshape(peers, slot, width)
    back = lax.all_to_all(result, "dp", split_axis=0, concat_axis=0, tiled=True)
    return back.reshape(-1, width)[target]


LAYERS, COLUMNS, CORES = 4, 2, 2
NEXT = (1, 3, 0, 2)
BACK = (2, 0, 3, 1)
STAY = (0, 1, 2, 3)


def moves(layers, column, core):
    return [
        (
            (z * COLUMNS + y) * CORES + c,
            (layers[z] * COLUMNS + (y ^ column)) * CORES + (c ^ core),
        )
        for z in range(LAYERS)
        for y in range(COLUMNS)
        for c in range(CORES)
    ]


def store_row(out_ref, n, at, row):
    high = row.astype(jnp.bfloat16)
    rest = row - high.astype(jnp.float32)
    middle = rest.astype(jnp.bfloat16)
    low = (rest - middle.astype(jnp.float32)).astype(jnp.bfloat16)
    out_ref[at:, :] = jnp.zeros((pad, out_ref.shape[1]), jnp.bfloat16)
    out_ref[at:, :n] = high
    out_ref[at:, n : 2 * n] = middle
    out_ref[at:, 2 * n : 3 * n] = low


def load_row(ref, n):
    at = ref.shape[0] - pad
    parts = ref[at:, : 3 * n].astype(jnp.float32)
    return parts[:1, :n] + parts[:1, n : 2 * n] + parts[:1, 2 * n : 3 * n]


def as_column(row):
    n = row.shape[1]
    return jnp.transpose(jnp.broadcast_to(row, (n, n)))[:, :1]


def as_rows(column):
    n = column.shape[0]
    return jnp.transpose(jnp.broadcast_to(column, (n, n)))[:pad, :]


def cat(values, axis=0):
    return jnp.concatenate(values, axis=axis)


def weights(units, ids, key_units, key_ids):
    gram = lax.dot_general(
        units, key_units, (((1,), (1,)), ((), ())), preferred_element_type=jnp.float32
    )
    weight = jnp.where(ids == key_ids, jnp.exp((gram - 1.0) / sharpness_scale), 0.0)
    return weight.astype(jnp.bfloat16), jnp.sum(weight, axis=1, keepdims=True)


def weighted(weight, rows):
    return jnp.dot(weight, rows, preferred_element_type=jnp.float32)


def join_body(rows, ids, out):
    n = rows.shape[0]
    out[:n, :] = rows[...]
    store_row(out, n, n, jnp.broadcast_to(ids[...].astype(jnp.float32), (pad, n)))


def load_body(rows, ids, near_rows, near_ids, sems):
    copies = [
        pltpu.make_async_copy(rows, near_rows, sems.at[0]),
        pltpu.make_async_copy(ids, near_ids, sems.at[1]),
    ]
    for copy in copies:
        copy.start()
    for copy in copies:
        copy.wait()


def split_body(rows, ids, out, first, second):
    n = rows.shape[0]
    half = n // 2
    row = jnp.broadcast_to(ids[...].astype(jnp.float32), (pad, n))
    out[:n, :] = rows[...]
    store_row(out, n, n, row)
    first[:half, :] = rows[:half, :]
    store_row(first, n, half, row)
    second[...] = rows[half:, :]


def reply_body(own, own2, col, col2, ring, own_ids, own2_ids, units, back):
    n = own.shape[0]
    blocks = (col, col2, ring)
    rows = [own[...], own2[...]] + [ref[:n, :] for ref in blocks]
    ids = [ref[...].astype(jnp.float32) for ref in (own_ids, own2_ids)]
    ids += [load_row(ref, n) for ref in blocks]
    parts = [normalize(r) for r in rows]
    weight, total = weights(parts[4], as_column(ids[4]), cat(parts[:4]), cat(ids[:4], 1))
    numer = weighted(weight, cat(rows[:4]))
    back[:n, :] = numer.astype(jnp.bfloat16)
    store_row(back, n, n, as_rows(total))
    for k, part in enumerate(parts):
        units[k * n : (k + 1) * n, :] = part


def rest_body(own, own2, col, col2, ring, ring2, own_ids, own2_ids, units, sums, totals):
    n = own.shape[0]
    blocks = (col, col2, ring, ring2)
    rows = [own[...], own2[...]] + [ref[:n, :] for ref in blocks]
    ids = [ref[...].astype(jnp.float32) for ref in (own_ids, own2_ids)]
    ids += [load_row(ref, n) for ref in blocks]
    weight, total = weights(
        units[:n, :], as_column(ids[0]), cat([units[...], normalize(rows[5])]), cat(ids, 1)
    )
    sums[...] = weighted(weight, cat(rows))
    totals[...] = jnp.broadcast_to(total, totals.shape)


def key_sums(unit, ids, keys):
    rows = cat([row for row, _ in keys])
    weight, total = weights(
        unit[: ids.shape[1], :], as_column(ids[...].astype(jnp.float32)), cat([normalize(row) for row, _ in keys]),
        cat([row for _, row in keys], 1),
    )
    return weighted(weight, rows), total


def keys_of(ref, n):
    return ref[:n, :], load_row(ref, n)


def first_of(ref, n):
    return ref[: n // 2, :], load_row(ref, n)[:, : n // 2]


def second_of(ref, first, n):
    return ref[...], load_row(first, n)[:, n // 2 :]


def add_to(sums, totals, new_sums, new_totals, unit, ids, keys):
    numer, total = key_sums(unit, ids, keys)
    new_sums[...] = sums[...] + numer
    new_totals[...] = totals[...] + total


def mid_body(unit, ids, sums, totals, side, side2, fa, fa2, new_sums, new_totals):
    n = ids.shape[1]
    keys = [keys_of(side, n), keys_of(side2, n), first_of(fa, n), first_of(fa2, n)]
    add_to(sums, totals, new_sums, new_totals, unit, ids, keys)


def late_body(unit, ids, sums, totals, fa, fa2, fb, fb2, sa, new_sums, new_totals):
    n = ids.shape[1]
    keys = [second_of(fb, fa, n), second_of(fb2, fa2, n), first_of(sa, n)]
    add_to(sums, totals, new_sums, new_totals, unit, ids, keys)


def last_body(unit, ids, sums, totals, sa, sa2, sb, new_sums, new_totals):
    n = ids.shape[1]
    keys = [first_of(sa2, n), second_of(sb, sa, n)]
    add_to(sums, totals, new_sums, new_totals, unit, ids, keys)


def finish_body(unit, ids, sums, totals, sa2, sb2, back, out, near_out, sems):
    n = ids.shape[1]
    numer, total = key_sums(unit, ids, [second_of(sb2, sa2, n)])
    scale = 1.0 / (total + totals[:, :1] + as_column(load_row(back, n)))
    step = n // 4
    copies = []
    for k in range(4):
        at = slice(k * step, (k + 1) * step)
        near_out[at, :] = (
            (numer[at] + sums[at, :] + back[at, :].astype(jnp.float32)) * scale[at]
        ).astype(jnp.bfloat16)
        here = pl.ds(k * step, step)
        copies.append(pltpu.make_async_copy(near_out.at[here], out.at[here], sems.at[k]))
        copies[-1].start()
    for copy in copies:
        copy.wait()


def call(body, outs, *args, in_space=pltpu.VMEM, out_space=pltpu.VMEM, scratch=()):
    kind = pltpu.VMEM if out_space is pltpu.VMEM else jax.ShapeDtypeStruct
    return pl.pallas_call(
        body,
        out_shape=[kind(shape, dtype) for shape, dtype in outs],
        in_specs=[pl.BlockSpec(memory_space=in_space)] * len(args),
        out_specs=[pl.BlockSpec(memory_space=out_space)] * len(outs),
        scratch_shapes=scratch,
        compiler_params=pltpu.CompilerParams(vmem_limit_bytes=24 * 2**20),
    )(*args)


def near(*arrays):
    return [pltpu.with_memory_space_constraint(x, pltpu.VMEM) for x in arrays]


def gathered(embeddings, cluster_ids):
    n, width = embeddings.shape
    half = n // 2
    f32, bf16 = jnp.float32, jnp.bfloat16

    def send(rows, layers, column, core):
        return lax.ppermute(rows, "dp", moves(layers, column, core))

    def swap(rows):
        return send(rows, STAY, 0, 1)

    def join(rows, ids):
        return call(join_body, [packet], *near(rows, ids))[0]

    packet = ((n + pad, width), bf16)
    own, ids = embeddings, cluster_ids[None, :]
    ring = send(own, NEXT, 0, 0)
    ring_ids = send(ids, NEXT, 0, 0)
    col = send(own, STAY, 1, 0)
    col_ids = send(ids, STAY, 1, 0)
    own2 = swap(own)
    own2_ids = swap(ids)
    own, ids = call(
        load_body, [((n, width), bf16), ((1, n), jnp.int32)], own, ids,
        in_space=pl.ANY, scratch=[pltpu.SemaphoreType.DMA((2,))],
    )
    ring, own = lax.optimization_barrier((ring, own))
    packet1, packet2 = ((half + pad, width), bf16), ((half, width), bf16)
    ring, ra, rb = call(split_body, [packet, packet1, packet2], *near(ring, ring_ids))
    fa = send(ra, NEXT, 0, 0)
    side = send(ring, STAY, 1, 0)
    ring2 = swap(ring)
    fb = send(rb, NEXT, 0, 0)
    col = join(col, col_ids)
    col2 = swap(col)

    state = [((n, width), f32), ((n, n), f32)]
    early = (own, own2, col, col2, ring)
    unit, back = call(reply_body, [((5 * n, width), bf16), packet], *near(*early, ids, own2_ids))
    fa, unit = lax.optimization_barrier((fa, unit))
    sa = send(fa, STAY, 1, 0)
    fa2 = swap(fa)
    back = send(back, BACK, 0, 0)
    sb = send(fb, STAY, 1, 0)
    fb2 = swap(fb)
    side2 = swap(side)
    fb, side, unit = lax.optimization_barrier((fb, side, unit))
    sums, totals = call(rest_body, state, *near(*early, ring2, ids, own2_ids, unit))
    side2, totals = lax.optimization_barrier((side2, totals))
    sums, totals = call(mid_body, state, *near(unit, ids, sums, totals, side, side2, fa, fa2))
    sa, totals = lax.optimization_barrier((sa, totals))
    sa2 = swap(sa)
    sums, totals = call(late_body, state, *near(unit, ids, sums, totals, fa, fa2, fb, fb2, sa))
    sb, totals = lax.optimization_barrier((sb, totals))
    sb2 = swap(sb)
    sums, totals = call(last_body, state, *near(unit, ids, sums, totals, sa, sa2, sb))
    out = ((n, width), bf16)
    return call(
        finish_body, [out], *near(unit, ids, sums, totals, sa2, sb2, back),
        out_space=pl.ANY, scratch=[pltpu.VMEM(*out), pltpu.SemaphoreType.DMA((4,))],
    )[0]


def shards(embeddings, cluster_ids, owner):
    if lax.axis_size("dp") == LAYERS * COLUMNS * CORES:
        return gathered(embeddings, cluster_ids)
    return exchange(embeddings, cluster_ids, owner)


def solution(mesh):
    placed = (P(("groups", "dp"), None), P(("groups", "dp")), P("groups"))
    return jax.shard_map(
        shards, mesh=mesh, in_specs=placed, out_specs=P(("groups", "dp"), None), check_vma=False
    )
```
